128 devices in a mesh: section: 8 (over z, y_hi), expert: 16 (over x, y_lo, core).
Axes of the slice: x: 4, y: 4 (y_hi: 2, y_lo: 2; y = y_hi * 2 + y_lo), z: 4, core: 2. Of those that a mesh axis runs over, the one named last changes fastest.
Arguments:
- activations: bfloat16 [8, 2048, 2048], P('section', 'expert'), may hold values from -6 to 6
- expert_ids: int32 [8, 8, 2048, 2], P('section', None, 'expert'), may hold values from 0 to 3, all different within a row; in each aligned block of 128 rows (0 to 127, 128 to 255, ..., all dimensions but the last counted through in order) at most 96 rows name the same one
- gate_values: bfloat16 [8, 8, 2048, 2], P('section', None, 'expert'), may hold values from 0.19921875 to 0.796875
- norm_gain: float32 [8, 2048], P('section'), may hold values from 0.1 to 1.9
- inner_weight: bfloat16 [8, 16, 2048, 2048], P('section', 'expert'), may hold values from -0.125 to 0.125
- outer_weight: bfloat16 [8, 16, 2048, 2048], P('section', 'expert'), may hold values from -0.0625 to 0.0625
Outputs:
- result: bfloat16 [8, 2048, 2048], P('section', 'expert')
The draws below stay inside these ranges and needn't reach their ends.
Inputs may be any that keep to these rules, and one draw needn't show every extreme that they name: `expert_ids`: each row names two different experts. Among the 128 rows of one device for one layer and micro-batch (aligned blocks), no expert is named more than 96 times, a bound that some block reaches in every draw.
All inputs are finite; a program needn't handle non-finite values.
Results may differ from the reference program's by a relative error of at most 0.0037.
Values may be sent and summed in bfloat16 or wider, within the bound.
No kernel may reach another device: no remote copies, remote signals or barrier semaphores. Data moves between devices by JAX's collectives and lax.ppermute only.
A program may use at most 128 MiB of HBM per device.

```python
import math
import jax
import jax.numpy as jnp
import numpy as np
from jax import lax

D = 2048
FF = 8192
SPLIT = 4
TICKS = 1
TOK_DEV = 128
LAYERS = 8
MB = 8
EXPERTS = 4
FF_DEV = 2048
TOKM = 2048
CAP = 96
N_EXPERT = 16


def shard_levels(own_key, dims, split, low, high):
    factor_of = 1.0
    for position, shards_of in split:
        steps = jax.random.uniform(jax.random.fold_in(jax.random.fold_in(own_key, 6), position), (shards_of,), jnp.float32, low / len(split), high / len(split))
        factor_of = factor_of * jnp.repeat(jnp.exp(steps), dims[position] // shards_of).reshape((-1,) + (1,) * (len(dims) - 1 - position))
    return factor_of


def assign_block(own_key, own, number, rows, number_of, top, limit, skew):
    order = jax.random.permutation(own_key, number_of)
    heavy_load, usual = load_shares(number_of, rows * top, limit, skew, True), load_shares(number_of, rows * top, limit, skew, False)
    places = jnp.arange(number_of)

    def named(tallies, turn):
        used = int((tallies > 0).sum())
        fixed = max(1, used // 4)
        passed = fixed + (places - fixed + turn * (used - fixed)) % max(1, number_of - fixed)
        return jnp.zeros((number_of,), jnp.int32).at[order[jnp.where(places < fixed, places, passed)]].set(jnp.asarray(tallies, jnp.int32))

    tallies = jnp.where(number % 4 == 0, named(heavy_load, number // 4), named(usual, number - number // 4 - 1))
    mixed = jax.random.permutation(jax.random.fold_in(own, 3), number_of)
    donor, taker = mixed[0:number_of // 2 * 2:2], mixed[1:number_of // 2 * 2:2]
    room = jnp.minimum(tallies[donor] - 1, limit - tallies[taker]) // 2
    room = jnp.where((donor == order[0]) | (taker == order[0]) | (tallies[taker] == 0), 0, jnp.maximum(room, 0))
    passed = jax.random.randint(jax.random.fold_in(own, 4), (number_of // 2,), 0, 1 << 20) % (room + 1)
    tallies = tallies.at[donor].add(-passed).at[taker].add(passed)
    members = jnp.searchsorted(jnp.cumsum(tallies), jnp.arange(rows * top), side="right").astype(jnp.int32)
    grid = members.reshape(top, rows).T
    grid = grid[jax.random.permutation(jax.random.fold_in(own, 1), rows)]
    turn = jax.random.randint(jax.random.fold_in(own, 2), (rows, 1), 0, top)
    return jnp.take_along_axis(grid, (jnp.arange(top)[None, :] + turn) % top, axis=1)


def load_shares(number_of, total, bound, slope, full):
    loads = [(1 << 20) // math.isqrt(grade ** slope) + 1 for grade in range(1, number_of + 1)]
    largest = bound if full else min(bound, max(-(-total // number_of), total * loads[0] // sum(loads)))
    least = 1 if total - largest >= number_of - 1 else 0
    given, surplus = [largest] + [least] * (number_of - 1), total - largest - least * (number_of - 1)
    while surplus > 0:
        candidates = [i for i in range(1, number_of) if given[i] < largest] or [i for i in range(1, number_of) if given[i] < bound]
        mass, left = sum([loads[i] for i in candidates]), surplus
        for i in candidates:
            extra = min(bound - given[i], max(1, left * loads[i] // mass), surplus)
            given[i] = given[i] + extra
            surplus = surplus - extra
    return np.array(given)


def scatter_about(stream_key, shape, deviation, bound, shards=(), kind=jnp.bfloat16):
    array = jax.random.normal(stream_key, shape, jnp.float32) * deviation
    if len(shards) > 0:
        array = shard_levels(stream_key, shape, shards, -0.22, 0.18) * array
    return jnp.clip(array, min=-bound, max=bound).astype(kind)


def setup_inputs(seed: int = 0) -> dict:
    splits = jax.random.split(jax.random.key(seed), 7)
    activations = scatter_about(splits[0], (MB, TOKM, D), 1.0, 6.0, ((0, 8), (1, 16)))
    expert_ids_keys = jax.random.split(jax.random.fold_in(splits[1], 1), LAYERS * MB * TOKM // TOK_DEV)
    expert_ids_turns = jax.random.permutation(jax.random.fold_in(splits[1], 3), LAYERS * MB * TOKM // TOK_DEV)
    expert_ids = jax.vmap(lambda own, number: assign_block(jax.random.fold_in(splits[1], 2), own, number, TOK_DEV, EXPERTS, 2, CAP, 2))(expert_ids_keys, expert_ids_turns).reshape((LAYERS, MB, TOKM, 2))
    gate_values = jnp.clip(0.19921875 + 0.59765625 * jax.random.uniform(splits[2], (LAYERS, MB, TOKM, 2), jnp.float32) ** shard_levels(splits[2], (LAYERS, MB, TOKM, 2), ((0, 8), (2, 16)), -0.2, 0.2), 0.19921875, 0.796875).astype(jnp.bfloat16)
    norm_gain = jnp.clip(1.0 + 0.18 * jax.random.normal(splits[3], (LAYERS, D), jnp.float32), 0.1, 1.9)
    inner_weight = scatter_about(splits[4], (LAYERS, N_EXPERT, D, FF_DEV), D ** -0.5, 0.125, ((0, 8), (1, 16)))
    outer_weight = scatter_about(splits[5], (LAYERS, N_EXPERT, FF_DEV, D), FF ** -0.5, 0.0625, ((0, 8), (1, 16)))
    return {"activations": activations, "expert_ids": expert_ids, "gate_values": gate_values, "norm_gain": norm_gain, "inner_weight": inner_weight, "outer_weight": outer_weight}


EPSILON = 1e-05

def slot_plan(block_ids, block_gates, expert_id, capacity):
    named_here = block_ids == expert_id
    member = lax.optimization_barrier(jnp.sum(named_here.astype(jnp.int32), axis=1))
    weight = lax.optimization_barrier(jnp.sum(jnp.where(named_here, block_gates.astype(jnp.float32), jnp.float32(0.0)), axis=1))
    slot_rank = jnp.cumsum(member) - 1
    slot_index = lax.broadcasted_iota(jnp.int32, (capacity, block_ids.shape[0]), 0)
    placement = jnp.where((slot_rank[None, :] == slot_index) & (member[None, :] == 1), jnp.float32(1.0), jnp.float32(0.0))
    slot_gate = lax.optimization_barrier(jnp.sum(placement * weight[None, :], axis=1))
    return (placement, slot_gate)

def layer_norm(carried, gain_row):
    widened = carried.astype(jnp.float32)
    row_mean = lax.optimization_barrier(jnp.mean(widened, axis=-1, keepdims=True))
    centred = widened - row_mean
    row_var = lax.optimization_barrier(jnp.mean(centred * centred, axis=-1, keepdims=True))
    return (centred * lax.rsqrt(row_var + EPSILON) * gain_row).astype(jnp.bfloat16)

def expert_forward(slot_rows, first_matrix, second_matrix):
    flat_rows = slot_rows.reshape(-1, slot_rows.shape[-1])
    hidden = jnp.maximum(jnp.dot(flat_rows, first_matrix, preferred_element_type=jnp.float32), 0.0).astype(jnp.bfloat16)
    layer_out = jnp.dot(hidden, second_matrix, preferred_element_type=jnp.float32)
    return layer_out.reshape(slot_rows.shape[:-1] + (second_matrix.shape[-1],))

def reference(activations, expert_ids, gate_values, norm_gain, inner_weight, outer_weight):

    def apply_layer(carried, layer_index, micro_batch):
        ids_layer = lax.dynamic_index_in_dim(expert_ids, layer_index, 0, keepdims=False)
        ids_now = lax.dynamic_index_in_dim(ids_layer, micro_batch, 0, keepdims=False)
        gates_layer = lax.dynamic_index_in_dim(gate_values, layer_index, 0, keepdims=False)
        gates_now = lax.dynamic_index_in_dim(gates_layer, micro_batch, 0, keepdims=False)
        gain_row = lax.dynamic_index_in_dim(norm_gain, layer_index, 0, keepdims=False)
        inner_layer = lax.dynamic_index_in_dim(inner_weight, layer_index, 0, keepdims=False)
        outer_layer = lax.dynamic_index_in_dim(outer_weight, layer_index, 0, keepdims=False)
        normed = layer_norm(carried, gain_row)
        block_rows = normed.reshape(N_EXPERT, TOK_DEV, D).astype(jnp.float32)
        block_ids = ids_now.reshape(N_EXPERT, TOK_DEV, 2)
        block_gates = gates_now.reshape(N_EXPERT, TOK_DEV, 2)
        branch = jnp.zeros((N_EXPERT, TOK_DEV, D), jnp.float32)
        for expert_id in range(EXPERTS):
            placement, slot_gate = jax.vmap(lambda ids_b, gates_b: slot_plan(ids_b, gates_b, expert_id, CAP))(block_ids, block_gates)
            slot_rows = jnp.einsum('sct,std->scd', placement, block_rows).astype(jnp.bfloat16)
            first_matrix = jnp.transpose(inner_layer[expert_id * SPLIT:(expert_id + 1) * SPLIT], (1, 0, 2)).reshape(D, FF)
            second_matrix = outer_layer[expert_id * SPLIT:(expert_id + 1) * SPLIT].reshape(FF, D)
            expert_out = expert_forward(slot_rows, first_matrix, second_matrix) * slot_gate[:, :, None]
            branch = branch + jnp.einsum('sct,scd->std', placement, expert_out, precision=lax.Precision.HIGHEST)
        return (carried.astype(jnp.float32) + branch.reshape(TOKM, D)).astype(jnp.bfloat16)

    def run_batch(micro_batch):

        def advance(offset, carried):
            return apply_layer(carried, (micro_batch + offset) % LAYERS, micro_batch)
        start_rows = lax.dynamic_index_in_dim(activations, micro_batch, 0, keepdims=False)
        return lax.fori_loop(0, TICKS, advance, start_rows)
    finished = lax.map(run_batch, jnp.arange(MB, dtype=jnp.int32))
    return jnp.roll(finished, TICKS, axis=0)
```

```python
import functools

import jax
import jax.numpy as jnp
from jax import lax
from jax.experimental import pallas as pl
from jax.experimental.pallas import tpu as pltpu
from jax.sharding import PartitionSpec as P


SPLIT = 4
EPSILON = 1e-05
OFFSETS = (0, 1, 3, 2)
NAMES = ("o", "p", "m", "t")
BF16 = jnp.bfloat16
F32 = jnp.float32


VMEM = pl.BlockSpec(memory_space=pltpu.VMEM)
SMEM = pl.BlockSpec(memory_space=pltpu.SMEM)
HBM = pl.BlockSpec(memory_space=pltpu.HBM)


def call(kernel, out, *args, scratch=(), smem=0, hbm=0, limit=10, flops=0):
    args = [
        pltpu.with_memory_space_constraint(arg, pltpu.HBM) if smem <= k < smem + hbm else arg
        for k, arg in enumerate(args)
    ]
    return pl.pallas_call(
        kernel,
        out_shape=out,
        in_specs=[SMEM] * smem + [HBM] * hbm + [VMEM] * (len(args) - smem - hbm),
        out_specs=jax.tree.map(lambda _: VMEM, out),
        scratch_shapes=scratch,
        compiler_params=pltpu.CompilerParams(vmem_limit_bytes=limit * 2**20),
        cost_estimate=pl.CostEstimate(
            flops=flops, bytes_accessed=1 << 20, transcendentals=0
        ),
    )(*args)


def ranks(ids, here):
    count = ids.shape[1]
    row = lax.broadcasted_iota(jnp.int32, (8, count), 0)
    offset = jnp.where(row == 2, 3, jnp.where(row == 3, 2, row))
    expert = jnp.where(row < 4, (here + offset) % 4, -1)
    named = (ids[0:1, :] == expert) | (ids[1:2, :] == expert)
    member = jnp.where(named, 1.0, 0.0).astype(BF16)
    earlier = lax.broadcasted_iota(jnp.int32, (count, count), 0) <= lax.broadcasted_iota(
        jnp.int32, (count, count), 1
    )
    upto = jnp.dot(member, jnp.where(earlier, 1.0, 0.0).astype(BF16), preferred_element_type=F32)
    return expert, jnp.where(named, upto - 1.0, -1.0)


def load_kernel(first_hbm, second_hbm, first_ref, second_ref, sems):
    copies = []
    for k, (source, target) in enumerate(((first_hbm, first_ref), (second_hbm, second_ref))):
        size = source.shape[0] // 4
        for j in range(4):
            cut = pl.ds(j * size, size)
            copies.append(pltpu.make_async_copy(source.at[cut], target.at[cut], sems.at[k, j]))
    for copy in copies:
        copy.start()
    for copy in copies:
        copy.wait()


def front_kernel(capacity, where_ref, rows_hbm, gain_hbm, ids_hbm, *refs):
    outs, (normed, pick, rows_ref, gain_ref, ids_ref, sems) = refs[:4], refs[4:]
    copies = [
        pltpu.make_async_copy(ids_hbm, ids_ref, sems.at[0]),
        pltpu.make_async_copy(rows_hbm, rows_ref, sems.at[1]),
        pltpu.make_async_copy(gain_hbm, gain_ref, sems.at[2]),
    ]
    for copy in copies:
        copy.start()
    copies[0].wait()
    count, width = rows_ref.shape
    _, slot = ranks(ids_ref[where_ref[0]], where_ref[1])
    index = lax.broadcasted_iota(jnp.int32, (capacity, count), 0).astype(F32)
    for k in range(4):
        pick[k * capacity : (k + 1) * capacity, :] = jnp.where(
            slot[k : k + 1, :] == index, 1.0, 0.0
        ).astype(BF16)
    copies[1].wait()
    copies[2].wait()
    for start in range(0, count, 16):
        part = rows_ref[start : start + 16, :].astype(F32)
        centred = part - jnp.mean(part, axis=-1, keepdims=True)
        spread = jnp.mean(centred * centred, axis=-1, keepdims=True)
        normed[start : start + 16, :] = (
            centred * lax.rsqrt(spread + EPSILON) * gain_ref[...]
        ).astype(BF16)
    for start in range(0, width, 512):
        part = jnp.dot(pick[...], normed[:, start : start + 512], preferred_element_type=F32)
        for k in range(4):
            outs[k][:, start : start + 512] = part[k * capacity : (k + 1) * capacity].astype(BF16)


def inner_kernel(a_ref, b_ref, c_ref, d_ref, weight_ref, hidden_ref, gathered):
    size = a_ref.shape[0]
    for k, ref in enumerate((a_ref, b_ref, c_ref, d_ref)):
        gathered[k * size : (k + 1) * size, :] = ref[...]
    for start in range(0, weight_ref.shape[1], 512):
        part = jnp.dot(
            gathered[...], weight_ref[:, start : start + 512], preferred_element_type=F32
        )
        hidden_ref[:, start : start + 512] = jnp.maximum(part, 0.0).astype(BF16)


def outer_kernel(hidden_ref, weight_ref, same_ref, side_ref, send_ref):
    size = same_ref.shape[0]
    for start in range(0, weight_ref.shape[1], 512):
        part = jnp.dot(
            hidden_ref[...], weight_ref[:, start : start + 512], preferred_element_type=F32
        )
        same_ref[:, start : start + 512] = part[:size]
        side_ref[:, start : start + 512] = part[size : 2 * size]
        send_ref[:, start : start + 512] = part[2 * size :].astype(BF16)


def side_kernel(side_ref, core_ref, out_ref):
    size = side_ref.shape[0]
    out_ref[...] = (side_ref[...] + core_ref[size:, :].astype(F32)).astype(BF16)


def same_kernel(same_ref, core_ref, other_ref, out_ref):
    size = same_ref.shape[0]
    out_ref[...] = (
        same_ref[...] + core_ref[:size, :].astype(F32) + other_ref[...].astype(F32)
    ).astype(BF16)


def own_kernel(
    capacity, where_ref, rows_ref, ids_ref, gates_ref, same_ref, core_ref, other_ref,
    p_ref, t_ref, sum_ref, last_ref, meta,
):
    count, width = rows_ref.shape
    ids = ids_ref[where_ref[0]]
    gates = gates_ref[where_ref[0]].astype(F32)
    expert, slot = ranks(ids, where_ref[1])
    gate = jnp.where(ids[0:1, :] == expert, gates[0:1, :], 0.0) + jnp.where(
        ids[1:2, :] == expert, gates[1:2, :], 0.0
    )
    meta[0:8, :] = slot
    meta[8:16, :] = gate
    eye = lax.broadcasted_iota(jnp.int32, (count, count), 0) == lax.broadcasted_iota(
        jnp.int32, (count, count), 1
    )
    turned = lax.dot_general(
        jnp.where(eye, 1.0, 0.0).astype(BF16),
        meta[...].astype(BF16),
        (((1,), (1,)), ((), ())),
        preferred_element_type=F32,
    )
    index = lax.broadcasted_iota(jnp.int32, (count, capacity), 1).astype(F32)

    def spread(k):
        return jnp.where(
            turned[:, k : k + 1] == index, turned[:, 8 + k : 9 + k], 0.0
        ).astype(BF16)

    own, plus, two = spread(0), spread(1), spread(3)
    last_ref[...] = spread(2)
    for start in range(0, width, 512):
        cut = slice(start, start + 512)
        local_rows = (
            same_ref[:, cut] + core_ref[:capacity, cut].astype(F32) + other_ref[:, cut].astype(F32)
        ).astype(BF16)
        sum_ref[:, cut] = (
            rows_ref[:, cut].astype(F32)
            + jnp.dot(own, local_rows, preferred_element_type=F32)
            + jnp.dot(plus, p_ref[:, cut], preferred_element_type=F32)
            + jnp.dot(two, t_ref[:, cut], preferred_element_type=F32)
        )


def last_kernel(sum_ref, last_ref, m_ref, out_ref):
    for start in range(0, sum_ref.shape[1], 512):
        cut = slice(start, start + 512)
        out_ref[:, cut] = (
            sum_ref[:, cut] + jnp.dot(last_ref[...], m_ref[:, cut], preferred_element_type=F32)
        ).astype(BF16)


def local(activations, expert_ids, gate_values, norm_gain, inner_weight, outer_weight):
    sections = lax.axis_size("section")
    owners = lax.axis_size("expert")
    rows = activations[0]
    count, width = rows.shape
    experts = owners // SPLIT
    capacity = min(count, 3 * count // experts)
    hidden_width = inner_weight.shape[-1]
    where = jnp.stack([lax.axis_index("section"), lax.axis_index("expert") // SPLIT])
    ids = jnp.swapaxes(expert_ids[0], 1, 2)
    gates = jnp.swapaxes(gate_values[0], 1, 2)

    def shape(size, kind=BF16, columns=width):
        return jax.ShapeDtypeStruct((size, columns), kind)

    def move(value, target):
        return lax.ppermute(value, "expert", [(i, target(i)) for i in range(owners)])

    def core(value):
        return move(value, lambda i: i ^ 1)

    def side(value):
        return move(value, lambda i: i ^ 2)

    def along(value, offset):
        return move(value, lambda i: (i + SPLIT * offset) % owners)

    slots = call(
        functools.partial(front_kernel, capacity),
        (shape(capacity),) * 4,
        where, rows, norm_gain, ids,
        smem=1,
        hbm=3,
        scratch=[
            pltpu.VMEM((count, width), BF16),
            pltpu.VMEM((4 * capacity, count), BF16),
            pltpu.VMEM((count, width), BF16),
            pltpu.VMEM(norm_gain.shape, F32),
            pltpu.VMEM(ids.shape, jnp.int32),
            pltpu.SemaphoreType.DMA((3,)),
        ],
    )
    first, second = call(
        load_kernel,
        (shape(width, columns=hidden_width), shape(hidden_width)),
        inner_weight[0, 0], outer_weight[0, 0],
        hbm=2,
        scratch=[pltpu.SemaphoreType.DMA((2, 4))],
    )
    kept = {}
    for name, offset, slot in zip(NAMES, OFFSETS, slots):
        mine = slot if offset == 0 else along(slot, offset)
        other = side(mine)
        hidden = call(
            inner_kernel,
            shape(4 * capacity, columns=hidden_width),
            mine, other, core(mine), core(other), first,
            scratch=[pltpu.VMEM((4 * capacity, width), BF16)],
            flops=8 * capacity * width * hidden_width,
        )
        same, across, send = call(
            outer_kernel,
            (shape(capacity, F32), shape(capacity, F32), shape(2 * capacity)),
            hidden, second,
            flops=8 * capacity * width * hidden_width,
        )
        back = core(send)
        give = call(side_kernel, shape(capacity), across, back)
        got = side(give)
        if offset == 0:
            kept[name] = (same, back, got)
        else:
            total = call(same_kernel, shape(capacity), same, back, got)
            kept[name] = along(total, -offset)
    partial, last = call(
        functools.partial(own_kernel, capacity),
        (shape(count, F32), shape(count, BF16, capacity)),
        where, rows, ids, gates, *kept["o"], kept["p"], kept["t"],
        smem=1,
        scratch=[pltpu.VMEM((16, count), F32)],
    )
    layer_out = call(last_kernel, shape(count), partial, last, kept["m"])
    moved = lax.ppermute(layer_out, "section", [(i, (i + 1) % sections) for i in range(sections)])
    return moved[None]


def solution(mesh):
    placed = (
        P("section", "expert", None),
        P("section", None, "expert", None),
        P("section", None, "expert", None),
        P("section", None),
        P("section", "expert", None, None),
        P("section", "expert", None, None),
    )
    return jax.shard_map(
        local, mesh=mesh, in_specs=placed, out_specs=P("section", "expert", None), check_vma=False
    )
```

```python
import functools

import jax
import jax.numpy as jnp
from jax import lax
from jax.experimental import pallas as pl
from jax.experimental.pallas import tpu as pltpu
from jax.sharding import PartitionSpec as P


SPLIT = 4
EPSILON = 1e-05
BF16 = jnp.bfloat16
F32 = jnp.float32


VMEM = pl.BlockSpec(memory_space=pltpu.VMEM)
SMEM = pl.BlockSpec(memory_space=pltpu.SMEM)
HBM = pl.BlockSpec(memory_space=pltpu.HBM)


def call(kernel, out, *args, scratch=(), smem=0, hbm=0, limit=10, flops=0):
    args = [
        pltpu.with_memory_space_constraint(arg, pltpu.HBM) if smem <= k < smem + hbm else arg
        for k, arg in enumerate(args)
    ]
    return pl.pallas_call(
        kernel,
        out_shape=out,
        in_specs=[SMEM] * smem + [HBM] * hbm + [VMEM] * (len(args) - smem - hbm),
        out_specs=jax.tree.map(lambda _: VMEM, out),
        scratch_shapes=scratch,
        compiler_params=pltpu.CompilerParams(vmem_limit_bytes=limit * 2**20),
        cost_estimate=pl.CostEstimate(
            flops=flops, bytes_accessed=1 << 20, transcendentals=0
        ),
    )(*args)


def ranks(ids, here):
    count = ids.shape[1]
    row = lax.broadcasted_iota(jnp.int32, (8, count), 0)
    offset = jnp.where(row == 2, 3, jnp.where(row == 3, 2, row))
    expert = jnp.where(row < 4, (here + offset) % 4, -1)
    named = (ids[0:1, :] == expert) | (ids[1:2, :] == expert)
    member = jnp.where(named, 1.0, 0.0).astype(BF16)
    earlier = lax.broadcasted_iota(jnp.int32, (count, count), 0) <= lax.broadcasted_iota(
        jnp.int32, (count, count), 1
    )
    upto = jnp.dot(member, jnp.where(earlier, 1.0, 0.0).astype(BF16), preferred_element_type=F32)
    return expert, jnp.where(named, upto - 1.0, -1.0)


def load_kernel(first_hbm, second_hbm, first_ref, second_ref, sems):
    copies = []
    for k, (source, target) in enumerate(((first_hbm, first_ref), (second_hbm, second_ref))):
        size = source.shape[0] // 4
        for j in range(4):
            cut = pl.ds(j * size, size)
            copies.append(pltpu.make_async_copy(source.at[cut], target.at[cut], sems.at[k, j]))
    for copy in copies:
        copy.start()
    for copy in copies:
        copy.wait()


def place(pick, slot, capacity, kinds):
    index = lax.broadcasted_iota(jnp.int32, (capacity, slot.shape[1]), 0).astype(F32)
    for k in range(kinds):
        pick[k * capacity : (k + 1) * capacity, :] = jnp.where(
            slot[k : k + 1, :] == index, 1.0, 0.0
        ).astype(BF16)


def gather(pick, rows_ref, outs, capacity):
    for start in range(0, rows_ref.shape[1], 512):
        part = jnp.dot(
            pick[...], rows_ref[: pick.shape[1], start : start + 512], preferred_element_type=F32
        )
        for k, out in enumerate(outs):
            out[:, start : start + 512] = part[k * capacity : (k + 1) * capacity].astype(BF16)


def front_kernel(capacity, where_ref, rows_hbm, gain_hbm, ids_hbm, gates_hbm, *refs):
    (tokens_ref, *outs), (pick, rows_ref, gain_ref, ids_ref, gates_ref, meta, sems) = (
        refs[:5], refs[5:],
    )
    copies = [
        pltpu.make_async_copy(source, target, sems.at[k])
        for k, (source, target) in enumerate(
            (
                (ids_hbm, ids_ref),
                (gates_hbm, gates_ref),
                (rows_hbm, rows_ref),
                (gain_hbm, gain_ref),
            )
        )
    ]
    for copy in copies:
        copy.start()
    count, width = rows_ref.shape
    copies[0].wait()
    copies[1].wait()
    ids = ids_ref[where_ref[0]]
    _, slot = ranks(ids, where_ref[1])
    place(pick, slot, capacity, 4)
    meta[...] = jnp.zeros_like(meta)
    meta[0:2, :] = ids.astype(F32)
    meta[2:4, :] = gates_ref[where_ref[0]].astype(F32)
    tokens_ref[count:, :] = jnp.zeros((8, width), BF16)
    tokens_ref[count:, 0:count] = meta[...].astype(BF16)
    copies[2].wait()
    copies[3].wait()
    for start in range(0, count, 16):
        part = rows_ref[start : start + 16, :].astype(F32)
        centred = part - jnp.mean(part, axis=-1, keepdims=True)
        spread = jnp.mean(centred * centred, axis=-1, keepdims=True)
        tokens_ref[start : start + 16, :] = (
            centred * lax.rsqrt(spread + EPSILON) * gain_ref[...]
        ).astype(BF16)
    gather(pick, tokens_ref, outs, capacity)


def cross_kernel(capacity, where_ref, tokens_ref, *refs):
    outs, (pick,) = refs[:3], refs[3:]
    count = pick.shape[1]
    ids = tokens_ref[count:, 0:count].astype(F32).astype(jnp.int32)
    _, slot = ranks(ids, where_ref[1])
    place(pick, slot, capacity, 3)
    gather(pick, tokens_ref, outs, capacity)


def spread(ids, gates, here, capacity, meta, outs):
    count = ids.shape[1]
    expert, slot = ranks(ids, here)
    meta[0:8, :] = slot
    meta[8:16, :] = jnp.where(ids[0:1, :] == expert, gates[0:1, :], 0.0) + jnp.where(
        ids[1:2, :] == expert, gates[1:2, :], 0.0
    )
    eye = lax.broadcasted_iota(jnp.int32, (count, count), 0) == lax.broadcasted_iota(
        jnp.int32, (count, count), 1
    )
    turned = lax.dot_general(
        jnp.where(eye, 1.0, 0.0).astype(BF16),
        meta[...].astype(BF16),
        (((1,), (1,)), ((), ())),
        preferred_element_type=F32,
    )
    index = lax.broadcasted_iota(jnp.int32, (count, capacity), 1).astype(F32)
    for k, out in enumerate(outs):
        out[...] = jnp.where(
            turned[:, k : k + 1] == index, turned[:, 8 + k : 9 + k], 0.0
        ).astype(BF16)


def plan_kernel(capacity, where_ref, ids_ref, gates_ref, tokens_ref, *refs):
    mine, theirs, meta = refs[:4], refs[4:7], refs[7]
    here = where_ref[1]
    gates = gates_ref[where_ref[0]].astype(F32)
    spread(ids_ref[where_ref[0]], gates, here, capacity, meta, mine)
    count = ids_ref.shape[2]
    packed = tokens_ref[count:, 0:count].astype(F32)
    spread(packed[0:2].astype(jnp.int32), packed[2:4], here, capacity, meta, theirs)


def inner_kernel(a_ref, b_ref, c_ref, d_ref, weight_ref, hidden_ref, gathered):
    size = a_ref.shape[0]
    for k, ref in enumerate((a_ref, b_ref, c_ref, d_ref)):
        gathered[k * size : (k + 1) * size, :] = ref[...]
    for start in range(0, weight_ref.shape[1], 512):
        part = jnp.dot(
            gathered[...], weight_ref[:, start : start + 512], preferred_element_type=F32
        )
        hidden_ref[:, start : start + 512] = jnp.maximum(part, 0.0).astype(BF16)


def outer_kernel(hidden_ref, weight_ref, same_ref, side_ref, send_ref):
    size = same_ref.shape[0]
    for start in range(0, weight_ref.shape[1], 512):
        part = jnp.dot(
            hidden_ref[...], weight_ref[:, start : start + 512], preferred_element_type=F32
        )
        same_ref[:, start : start + 512] = part[:size]
        side_ref[:, start : start + 512] = part[size : 2 * size]
        send_ref[:, start : start + 512] = part[2 * size :].astype(BF16)


def side_kernel(side_ref, core_ref, out_ref):
    size = side_ref.shape[0]
    out_ref[...] = (side_ref[...] + core_ref[size:, :].astype(F32)).astype(BF16)


def both_kernel(same_ref, side_ref, core_ref, one_ref, two_ref):
    size = side_ref.shape[0]
    one_ref[...] = (same_ref[...] + core_ref[:size, :].astype(F32)).astype(BF16)
    two_ref[...] = (side_ref[...] + core_ref[size:, :].astype(F32)).astype(BF16)


def same_kernel(same_ref, core_ref, other_ref, out_ref):
    size = same_ref.shape[0]
    out_ref[...] = (
        same_ref[...] + core_ref[:size, :].astype(F32) + other_ref[...].astype(F32)
    ).astype(BF16)


def theirs_kernel(base, o_ref, p_ref, m_ref, side_ref, core_ref, zp_ref, zm_ref, out_ref):
    size = side_ref.shape[0]
    for start in range(0, out_ref.shape[1], 512):
        cut = slice(base + start, base + start + 512)
        here = (side_ref[:, cut] + core_ref[size:, cut].astype(F32)).astype(BF16)
        out_ref[:, start : start + 512] = (
            jnp.dot(o_ref[...], here, preferred_element_type=F32)
            + jnp.dot(p_ref[...], zp_ref[:, cut], preferred_element_type=F32)
            + jnp.dot(m_ref[...], zm_ref[:, cut], preferred_element_type=F32)
        ).astype(BF16)


def own_kernel(rows_ref, o_ref, p_ref, m_ref, same_ref, core_ref, wp_ref, wm_ref, sum_ref):
    size = same_ref.shape[0]
    for start in range(0, sum_ref.shape[1], 512):
        cut = slice(start, start + 512)
        here = (same_ref[:, cut] + core_ref[:size, cut].astype(F32)).astype(BF16)
        sum_ref[:, cut] = (
            rows_ref[:, cut].astype(F32)
            + jnp.dot(o_ref[...], here, preferred_element_type=F32)
            + jnp.dot(p_ref[...], wp_ref[:, cut], preferred_element_type=F32)
            + jnp.dot(m_ref[...], wm_ref[:, cut], preferred_element_type=F32)
        )


def last_kernel(base, sum_ref, t_ref, wt_ref, across_ref, out_ref):
    for start in range(0, out_ref.shape[1], 512):
        cut = slice(base + start, base + start + 512)
        out_ref[:, start : start + 512] = (
            sum_ref[:, cut]
            + jnp.dot(t_ref[...], wt_ref[:, cut], preferred_element_type=F32)
            + across_ref[:, start : start + 512].astype(F32)
        ).astype(BF16)


def local(activations, expert_ids, gate_values, norm_gain, inner_weight, outer_weight):
    sections = lax.axis_size("section")
    owners = lax.axis_size("expert")
    rows = activations[0]
    count, width = rows.shape
    experts = owners // SPLIT
    capacity = min(count, 3 * count // experts)
    hidden_width = inner_weight.shape[-1]
    where = jnp.stack([lax.axis_index("section"), lax.axis_index("expert") // SPLIT])
    ids = jnp.swapaxes(expert_ids[0], 1, 2)
    gates = jnp.swapaxes(gate_values[0], 1, 2)

    def shape(size, kind=BF16, columns=width):
        return jax.ShapeDtypeStruct((size, columns), kind)

    def move(value, target):
        return lax.ppermute(value, "expert", [(i, target(i)) for i in range(owners)])

    def core(value):
        return move(value, lambda i: i ^ 1)

    def side(value):
        return move(value, lambda i: i ^ 2)

    def along(value, offset):
        return move(value, lambda i: (i + SPLIT * offset) % owners)

    tokens, *slots = call(
        functools.partial(front_kernel, capacity),
        (shape(count + 8),) + (shape(capacity),) * 4,
        where, rows, norm_gain, ids, gates,
        smem=1,
        hbm=4,
        scratch=[
            pltpu.VMEM((4 * capacity, count), BF16),
            pltpu.VMEM((count, width), BF16),
            pltpu.VMEM(norm_gain.shape, F32),
            pltpu.VMEM(ids.shape, jnp.int32),
            pltpu.VMEM(gates.shape, BF16),
            pltpu.VMEM((8, count), F32),
            pltpu.SemaphoreType.DMA((4,)),
        ],
    )
    first, second = call(
        load_kernel,
        (shape(width, columns=hidden_width), shape(hidden_width)),
        inner_weight[0, 0], outer_weight[0, 0],
        hbm=2,
        scratch=[pltpu.SemaphoreType.DMA((2, 4))],
    )
    o_slots, p_slots, m_slots, t_slots = slots
    others = side(tokens)
    o_cross, p_cross, m_cross = call(
        functools.partial(cross_kernel, capacity),
        (shape(capacity),) * 3,
        where, others,
        smem=1,
        scratch=[pltpu.VMEM((3 * capacity, count), BF16)],
    )
    plans = call(
        functools.partial(plan_kernel, capacity),
        (shape(count, BF16, capacity),) * 7,
        where, ids, gates, others,
        smem=1,
        scratch=[pltpu.VMEM((16, count), F32)],
    )

    def experts_of(one, two):
        hidden = call(
            inner_kernel,
            shape(4 * capacity, columns=hidden_width),
            one, two, core(one), core(two), first,
            scratch=[pltpu.VMEM((4 * capacity, width), BF16)],
            flops=8 * capacity * width * hidden_width,
        )
        same, across, send = call(
            outer_kernel,
            (shape(capacity, F32), shape(capacity, F32), shape(2 * capacity)),
            hidden, second,
            flops=8 * capacity * width * hidden_width,
        )
        return same, across, core(send)

    two_on = along(t_slots, 2)
    same, across, back = experts_of(two_on, side(two_on))
    got = side(call(side_kernel, shape(capacity), across, back))
    t_back = along(call(same_kernel, shape(capacity), same, back, got), -2)

    plus, minus = along(p_slots, 1), along(m_slots, -1)
    parts = experts_of(plus, minus)
    plus, minus = call(both_kernel, (shape(capacity),) * 2, *parts)
    p_back, m_back = along(plus, -1), along(minus, 1)

    plus, minus = along(p_cross, 1), along(m_cross, -1)
    parts = experts_of(plus, minus)
    plus, minus = call(both_kernel, (shape(capacity),) * 2, *parts)
    p_other, m_other = along(plus, -1), along(minus, 1)

    same, across, back = experts_of(o_slots, o_cross)
    partial = call(own_kernel, shape(count, F32), rows, *plans[:3], same, back, p_back, m_back)
    half = width // 2
    pieces = []
    for k in range(2):
        across_sum = call(
            functools.partial(theirs_kernel, k * half),
            shape(count, columns=half),
            *plans[4:7], across, back, p_other, m_other,
        )
        arrived = side(across_sum)
        layer_out = call(
            functools.partial(last_kernel, k * half),
            shape(count, columns=half),
            partial, plans[3], t_back, arrived,
        )
        pieces.append(
            lax.ppermute(layer_out, "section", [(i, (i + 1) % sections) for i in range(sections)])
        )
    return jnp.concatenate(pieces, axis=1)[None]


def solution(mesh):
    placed = (
        P("section", "expert", None),
        P("section", None, "expert", None),
        P("section", None, "expert", None),
        P("section", None),
        P("section", "expert", None, None),
        P("section", "expert", None, None),
    )
    return jax.shard_map(
        local, mesh=mesh, in_specs=placed, out_specs=P("section", "expert", None), check_vma=False
    )
```

```python
import functools

import jax
import jax.numpy as jnp
from jax import lax
from jax.experimental import pallas as pl
from jax.experimental.pallas import tpu as pltpu
from jax.sharding import PartitionSpec as P


SPLIT = 4
EPSILON = 1e-05
OFFSETS = (0, 1, 3, 2)
NAMES = ("o", "p", "m", "t")
BF16 = jnp.bfloat16
F32 = jnp.float32


VMEM = pl.BlockSpec(memory_space=pltpu.VMEM)
SMEM = pl.BlockSpec(memory_space=pltpu.SMEM)
HBM = pl.BlockSpec(memory_space=pltpu.HBM)


def call(kernel, out, *args, scratch=(), smem=0, hbm=0, limit=10, flops=0):
    args = [
        pltpu.with_memory_space_constraint(arg, pltpu.HBM) if smem <= k < smem + hbm else arg
        for k, arg in enumerate(args)
    ]
    return pl.pallas_call(
        kernel,
        out_shape=out,
        in_specs=[SMEM] * smem + [HBM] * hbm + [VMEM] * (len(args) - smem - hbm),
        out_specs=jax.tree.map(lambda _: VMEM, out),
        scratch_shapes=scratch,
        compiler_params=pltpu.CompilerParams(vmem_limit_bytes=limit * 2**20),
        cost_estimate=pl.CostEstimate(
            flops=flops, bytes_accessed=1 << 20, transcendentals=0
        ),
    )(*args)


def ranks(ids, here):
    count = ids.shape[1]
    row = lax.broadcasted_iota(jnp.int32, (8, count), 0)
    offset = jnp.where(row == 2, 3, jnp.where(row == 3, 2, row))
    expert = jnp.where(row < 4, (here + offset) % 4, -1)
    named = (ids[0:1, :] == expert) | (ids[1:2, :] == expert)
    member = jnp.where(named, 1.0, 0.0).astype(BF16)
    earlier = lax.broadcasted_iota(jnp.int32, (count, count), 0) <= lax.broadcasted_iota(
        jnp.int32, (count, count), 1
    )
    upto = jnp.dot(member, jnp.where(earlier, 1.0, 0.0).astype(BF16), preferred_element_type=F32)
    return expert, jnp.where(named, upto - 1.0, -1.0)


def load_kernel(source, target, sems):
    size = source.shape[0] // 4
    cuts = [pl.ds(j * size, size) for j in range(4)]
    copies = [
        pltpu.make_async_copy(source.at[cut], target.at[cut], sems.at[j])
        for j, cut in enumerate(cuts)
    ]
    for copy in copies:
        copy.start()
    for copy in copies:
        copy.wait()


def front_kernel(capacity, where_ref, rows_hbm, gain_hbm, ids_hbm, *refs):
    outs, (normed, pick, rows_ref, gain_ref, ids_ref, sems) = refs[:4], refs[4:]
    copies = [
        pltpu.make_async_copy(ids_hbm, ids_ref, sems.at[0]),
        pltpu.make_async_copy(rows_hbm, rows_ref, sems.at[1]),
        pltpu.make_async_copy(gain_hbm, gain_ref, sems.at[2]),
    ]
    for copy in copies:
        copy.start()
    copies[0].wait()
    count, width = rows_ref.shape
    _, slot = ranks(ids_ref[where_ref[0]], where_ref[1])
    index = lax.broadcasted_iota(jnp.int32, (capacity, count), 0).astype(F32)
    for k in range(4):
        pick[k * capacity : (k + 1) * capacity, :] = jnp.where(
            slot[k : k + 1, :] == index, 1.0, 0.0
        ).astype(BF16)
    copies[1].wait()
    copies[2].wait()
    for start in range(0, count, 16):
        part = rows_ref[start : start + 16, :].astype(F32)
        centred = part - jnp.mean(part, axis=-1, keepdims=True)
        spread = jnp.mean(centred * centred, axis=-1, keepdims=True)
        normed[start : start + 16, :] = (
            centred * lax.rsqrt(spread + EPSILON) * gain_ref[...]
        ).astype(BF16)
    for start in range(0, width, 512):
        part = jnp.dot(pick[...], normed[:, start : start + 512], preferred_element_type=F32)
        for k in range(4):
            outs[k][:, start : start + 512] = part[k * capacity : (k + 1) * capacity].astype(BF16)


def inner_kernel(a_ref, b_ref, c_ref, d_ref, weight_ref, hidden_ref, gathered):
    size = a_ref.shape[0]
    for k, ref in enumerate((a_ref, b_ref, c_ref, d_ref)):
        gathered[k * size : (k + 1) * size, :] = ref[...]
    for start in range(0, weight_ref.shape[1], 512):
        part = jnp.dot(
            gathered[...], weight_ref[:, start : start + 512], preferred_element_type=F32
        )
        hidden_ref[:, start : start + 512] = jnp.maximum(part, 0.0).astype(BF16)


def outer_kernel(hidden_ref, weight_ref, same_ref, side_ref, send_ref):
    size = same_ref.shape[0]
    for start in range(0, weight_ref.shape[1], 512):
        part = jnp.dot(
            hidden_ref[...], weight_ref[:, start : start + 512], preferred_element_type=F32
        )
        same_ref[:, start : start + 512] = part[:size]
        side_ref[:, start : start + 512] = part[size : 2 * size]
        send_ref[:, start : start + 512] = part[2 * size :].astype(BF16)


def side_kernel(side_ref, core_ref, out_ref):
    size = side_ref.shape[0]
    out_ref[...] = (side_ref[...] + core_ref[size:, :].astype(F32)).astype(BF16)


def same_kernel(same_ref, core_ref, other_ref, out_ref):
    size = same_ref.shape[0]
    out_ref[...] = (
        same_ref[...] + core_ref[:size, :].astype(F32) + other_ref[...].astype(F32)
    ).astype(BF16)


def side_halves_kernel(side_ref, core_ref, *out_refs):
    size = side_ref.shape[0]
    half = size // 2
    for k, out_ref in enumerate(out_refs):
        cut = slice(k * half, (k + 1) * half)
        above = slice(size + k * half, size + (k + 1) * half)
        out_ref[...] = (side_ref[cut, :] + core_ref[above, :].astype(F32)).astype(BF16)


def same_half_kernel(base, same_ref, core_ref, other_ref, out_ref):
    cut = slice(base, base + other_ref.shape[0])
    out_ref[...] = (
        same_ref[cut, :] + core_ref[cut, :].astype(F32) + other_ref[...].astype(F32)
    ).astype(BF16)


def own_kernel(
    capacity, where_ref, rows_ref, ids_ref, gates_ref, p_ref, t_ref,
    sum_ref, own_ref, one_ref, two_ref, meta,
):
    count, width = rows_ref.shape
    ids = ids_ref[where_ref[0]]
    gates = gates_ref[where_ref[0]].astype(F32)
    expert, slot = ranks(ids, where_ref[1])
    gate = jnp.where(ids[0:1, :] == expert, gates[0:1, :], 0.0) + jnp.where(
        ids[1:2, :] == expert, gates[1:2, :], 0.0
    )
    meta[0:8, :] = slot
    meta[8:16, :] = gate
    eye = lax.broadcasted_iota(jnp.int32, (count, count), 0) == lax.broadcasted_iota(
        jnp.int32, (count, count), 1
    )
    turned = lax.dot_general(
        jnp.where(eye, 1.0, 0.0).astype(BF16),
        meta[...].astype(BF16),
        (((1,), (1,)), ((), ())),
        preferred_element_type=F32,
    )
    index = lax.broadcasted_iota(jnp.int32, (count, capacity), 1).astype(F32)
    half = capacity // 2
    early = lax.broadcasted_iota(jnp.int32, (count, half), 1).astype(F32)

    def spread(k, slots):
        return jnp.where(
            turned[:, k : k + 1] == slots, turned[:, 8 + k : 9 + k], 0.0
        ).astype(BF16)

    plus, two = spread(1, index), spread(3, index)
    own_ref[...] = spread(0, index)
    one_ref[...] = spread(2, early)
    two_ref[...] = spread(2, early + half)
    for start in range(0, width, 512):
        cut = slice(start, start + 512)
        sum_ref[:, cut] = (
            rows_ref[:, cut].astype(F32)
            + jnp.dot(plus, p_ref[:, cut], preferred_element_type=F32)
            + jnp.dot(two, t_ref[:, cut], preferred_element_type=F32)
        )


def last_kernel(
    sum_ref, own_ref, one_ref, two_ref, same_ref, core_ref, other_ref, m1_ref, m2_ref, out_ref
):
    capacity = other_ref.shape[0]
    for start in range(0, sum_ref.shape[1], 512):
        cut = slice(start, start + 512)
        local_rows = (
            same_ref[:, cut] + core_ref[:capacity, cut].astype(F32) + other_ref[:, cut].astype(F32)
        ).astype(BF16)
        out_ref[0, :, cut] = (
            sum_ref[:, cut]
            + jnp.dot(own_ref[...], local_rows, preferred_element_type=F32)
            + jnp.dot(one_ref[...], m1_ref[:, cut], preferred_element_type=F32)
            + jnp.dot(two_ref[...], m2_ref[:, cut], preferred_element_type=F32)
        ).astype(BF16)


def local(activations, expert_ids, gate_values, norm_gain, inner_weight, outer_weight):
    sections = lax.axis_size("section")
    owners = lax.axis_size("expert")
    rows = activations[0]
    count, width = rows.shape
    experts = owners // SPLIT
    capacity = min(count, 3 * count // experts)
    hidden_width = inner_weight.shape[-1]
    where = jnp.stack([lax.axis_index("section"), lax.axis_index("expert") // SPLIT])
    ids = jnp.swapaxes(expert_ids[0], 1, 2)
    gates = jnp.swapaxes(gate_values[0], 1, 2)

    def shape(size, kind=BF16, columns=width):
        return jax.ShapeDtypeStruct((size, columns), kind)

    def move(value, target):
        return lax.ppermute(value, "expert", [(i, target(i)) for i in range(owners)])

    def core(value):
        return move(value, lambda i: i ^ 1)

    def side(value):
        return move(value, lambda i: i ^ 2)

    def along(value, offset):
        return move(value, lambda i: (i + SPLIT * offset) % owners)

    slots = call(
        functools.partial(front_kernel, capacity),
        (shape(capacity),) * 4,
        where, rows, norm_gain, ids,
        smem=1,
        hbm=3,
        scratch=[
            pltpu.VMEM((count, width), BF16),
            pltpu.VMEM((4 * capacity, count), BF16),
            pltpu.VMEM((count, width), BF16),
            pltpu.VMEM(norm_gain.shape, F32),
            pltpu.VMEM(ids.shape, jnp.int32),
            pltpu.SemaphoreType.DMA((3,)),
        ],
    )
    first, second = (
        call(load_kernel, shape(weight.shape[0], columns=weight.shape[1]), weight,
             hbm=1, scratch=[pltpu.SemaphoreType.DMA((4,))])
        for weight in (inner_weight[0, 0], outer_weight[0, 0])
    )
    kept = {}
    for name, offset, slot in zip(NAMES, OFFSETS, slots):
        mine = slot if offset == 0 else along(slot, offset)
        other = side(mine)
        hidden = call(
            inner_kernel,
            shape(4 * capacity, columns=hidden_width),
            mine, other, core(mine), core(other), first,
            scratch=[pltpu.VMEM((4 * capacity, width), BF16)],
            flops=8 * capacity * width * hidden_width,
        )
        same, across, send = call(
            outer_kernel,
            (shape(capacity, F32), shape(capacity, F32), shape(2 * capacity)),
            hidden, second,
            flops=8 * capacity * width * hidden_width,
        )
        back = core(send)
        if name == "m":
            half = capacity // 2
            gives = call(side_halves_kernel, (shape(half),) * 2, across, back)
            kept[name] = [
                along(
                    call(
                        functools.partial(same_half_kernel, k * half),
                        shape(half),
                        same, back, side(give),
                    ),
                    -offset,
                )
                for k, give in enumerate(gives)
            ]
            continue
        got = side(call(side_kernel, shape(capacity), across, back))
        if name == "o":
            kept[name] = (same, back, got)
        else:
            total = call(same_kernel, shape(capacity), same, back, got)
            kept[name] = along(total, -offset)
    partial, *spreads = call(
        functools.partial(own_kernel, capacity),
        (
            shape(count, F32), shape(count, BF16, capacity),
            shape(count, BF16, capacity // 2), shape(count, BF16, capacity // 2),
        ),
        where, rows, ids, gates, kept["p"], kept["t"],
        smem=1,
        scratch=[pltpu.VMEM((16, count), F32)],
    )
    layer_out = call(
        last_kernel,
        jax.ShapeDtypeStruct((1, count, width), BF16),
        partial, *spreads, *kept["o"], *kept["m"],
    )
    moved = lax.ppermute(layer_out, "section", [(i, (i + 1) % sections) for i in range(sections)])
    return moved


def solution(mesh):
    placed = (
        P("section", "expert", None),
        P("section", None, "expert", None),
        P("section", None, "expert", None),
        P("section", None),
        P("section", "expert", None, None),
        P("section", "expert", None, None),
    )
    return jax.shard_map(
        local, mesh=mesh, in_specs=placed, out_specs=P("section", "expert", None), check_vma=False
    )
```

```python
import functools

import jax
import jax.numpy as jnp
from jax import lax
from jax.experimental import pallas as pl
from jax.experimental.pallas import tpu as pltpu
from jax.sharding import PartitionSpec as P


SPLIT = 4
EPSILON = 1e-05
BF16 = jnp.bfloat16
F32 = jnp.float32


VMEM = pl.BlockSpec(memory_space=pltpu.VMEM)
SMEM = pl.BlockSpec(memory_space=pltpu.SMEM)
HBM = pl.BlockSpec(memory_space=pltpu.HBM)


def call(kernel, out, *args, scratch=(), smem=0, hbm=0, limit=10, flops=0):
    args = [
        pltpu.with_memory_space_constraint(arg, pltpu.HBM) if smem <= k < smem + hbm else arg
        for k, arg in enumerate(args)
    ]
    return pl.pallas_call(
        kernel,
        out_shape=out,
        in_specs=[SMEM] * smem + [HBM] * hbm + [VMEM] * (len(args) - smem - hbm),
        out_specs=jax.tree.map(lambda _: VMEM, out),
        scratch_shapes=scratch,
        compiler_params=pltpu.CompilerParams(vmem_limit_bytes=limit * 2**20),
        cost_estimate=pl.CostEstimate(
            flops=flops, bytes_accessed=1 << 20, transcendentals=0
        ),
    )(*args)


def ranks(ids, here):
    count = ids.shape[1]
    row = lax.broadcasted_iota(jnp.int32, (8, count), 0)
    offset = jnp.where(row == 2, 3, jnp.where(row == 3, 2, row))
    expert = jnp.where(row < 4, (here + offset) % 4, -1)
    named = (ids[0:1, :] == expert) | (ids[1:2, :] == expert)
    member = jnp.where(named, 1.0, 0.0).astype(BF16)
    earlier = lax.broadcasted_iota(jnp.int32, (count, count), 0) <= lax.broadcasted_iota(
        jnp.int32, (count, count), 1
    )
    upto = jnp.dot(member, jnp.where(earlier, 1.0, 0.0).astype(BF16), preferred_element_type=F32)
    return expert, jnp.where(named, upto - 1.0, -1.0)


def load_kernel(first_hbm, second_hbm, first_ref, second_ref, sems):
    copies = []
    for k, (source, target) in enumerate(((first_hbm, first_ref), (second_hbm, second_ref))):
        size = source.shape[0] // 4
        for j in range(4):
            cut = pl.ds(j * size, size)
            copies.append(pltpu.make_async_copy(source.at[cut], target.at[cut], sems.at[k, j]))
    for copy in copies:
        copy.start()
    for copy in copies:
        copy.wait()


def place(pick, slot, capacity, kinds):
    index = lax.broadcasted_iota(jnp.int32, (capacity, slot.shape[1]), 0).astype(F32)
    for k in range(kinds):
        pick[k * capacity : (k + 1) * capacity, :] = jnp.where(
            slot[k : k + 1, :] == index, 1.0, 0.0
        ).astype(BF16)


def gather(pick, rows_ref, outs, capacity):
    for start in range(0, rows_ref.shape[1], 512):
        part = jnp.dot(
            pick[...], rows_ref[: pick.shape[1], start : start + 512], preferred_element_type=F32
        )
        for k, out in enumerate(outs):
            out[:, start : start + 512] = part[k * capacity : (k + 1) * capacity].astype(BF16)


def front_kernel(capacity, where_ref, rows_hbm, gain_hbm, ids_hbm, gates_hbm, *refs):
    (tokens_ref, *outs), (pick, rows_ref, gain_ref, ids_ref, gates_ref, meta, sems) = (
        refs[:5], refs[5:],
    )
    copies = [
        pltpu.make_async_copy(source, target, sems.at[k])
        for k, (source, target) in enumerate(
            (
                (ids_hbm, ids_ref),
                (gates_hbm, gates_ref),
                (rows_hbm, rows_ref),
                (gain_hbm, gain_ref),
            )
        )
    ]
    for copy in copies:
        copy.start()
    count, width = rows_ref.shape
    copies[0].wait()
    copies[1].wait()
    ids = ids_ref[where_ref[0]]
    _, slot = ranks(ids, where_ref[1])
    place(pick, slot, capacity, 4)
    meta[...] = jnp.zeros_like(meta)
    meta[0:2, :] = ids.astype(F32)
    meta[2:4, :] = gates_ref[where_ref[0]].astype(F32)
    tokens_ref[count:, :] = jnp.zeros((8, width), BF16)
    tokens_ref[count:, 0:count] = meta[...].astype(BF16)
    copies[2].wait()
    copies[3].wait()
    for start in range(0, count, 16):
        part = rows_ref[start : start + 16, :].astype(F32)
        centred = part - jnp.mean(part, axis=-1, keepdims=True)
        spread = jnp.mean(centred * centred, axis=-1, keepdims=True)
        tokens_ref[start : start + 16, :] = (
            centred * lax.rsqrt(spread + EPSILON) * gain_ref[...]
        ).astype(BF16)
    gather(pick, tokens_ref, outs, capacity)


def cross_kernel(capacity, where_ref, tokens_ref, *refs):
    outs, (pick,) = refs[:3], refs[3:]
    count = pick.shape[1]
    ids = tokens_ref[count:, 0:count].astype(F32).astype(jnp.int32)
    _, slot = ranks(ids, where_ref[1])
    place(pick, slot, capacity, 3)
    gather(pick, tokens_ref, outs, capacity)


def inner_kernel(a_ref, b_ref, c_ref, d_ref, weight_ref, hidden_ref, gathered):
    size = a_ref.shape[0]
    for k, ref in enumerate((a_ref, b_ref, c_ref, d_ref)):
        gathered[k * size : (k + 1) * size, :] = ref[...]
    for start in range(0, weight_ref.shape[1], 512):
        part = jnp.dot(
            gathered[...], weight_ref[:, start : start + 512], preferred_element_type=F32
        )
        hidden_ref[:, start : start + 512] = jnp.maximum(part, 0.0).astype(BF16)


def outer_kernel(hidden_ref, weight_ref, same_ref, side_ref, send_ref):
    size = same_ref.shape[0]
    for start in range(0, weight_ref.shape[1], 512):
        part = jnp.dot(
            hidden_ref[...], weight_ref[:, start : start + 512], preferred_element_type=F32
        )
        same_ref[:, start : start + 512] = part[:size]
        side_ref[:, start : start + 512] = part[size : 2 * size]
        send_ref[:, start : start + 512] = part[2 * size :].astype(BF16)


def side_kernel(side_ref, core_ref, out_ref):
    size = side_ref.shape[0]
    out_ref[...] = (side_ref[...] + core_ref[size:, :].astype(F32)).astype(BF16)


def same_kernel(same_ref, core_ref, other_ref, out_ref):
    size = same_ref.shape[0]
    out_ref[...] = (
        same_ref[...] + core_ref[:size, :].astype(F32) + other_ref[...].astype(F32)
    ).astype(BF16)


def cross_sums_kernel(plus_ref, minus_ref, core_ref, out_ref, one_ref, two_ref):
    size = plus_ref.shape[0]
    half = size // 2
    out_ref[...] = (plus_ref[...] + core_ref[:size, :].astype(F32)).astype(BF16)
    for k, half_ref in enumerate((one_ref, two_ref)):
        cut = slice(k * half, (k + 1) * half)
        below = slice(size + k * half, size + (k + 1) * half)
        half_ref[...] = (minus_ref[cut, :] + core_ref[below, :].astype(F32)).astype(BF16)


def minus_half_kernel(base, minus_ref, core_ref, other_ref, out_ref):
    size, half = minus_ref.shape[0], other_ref.shape[0]
    out_ref[...] = (
        minus_ref[base : base + half, :]
        + core_ref[size + base : size + base + half, :].astype(F32)
        + other_ref[...].astype(F32)
    ).astype(BF16)


def own_kernel(
    capacity, where_ref, rows_ref, ids_ref, gates_ref, t_ref,
    sum_ref, own_ref, plus_ref, one_ref, two_ref, meta,
):
    count, width = rows_ref.shape
    ids = ids_ref[where_ref[0]]
    gates = gates_ref[where_ref[0]].astype(F32)
    expert, slot = ranks(ids, where_ref[1])
    gate = jnp.where(ids[0:1, :] == expert, gates[0:1, :], 0.0) + jnp.where(
        ids[1:2, :] == expert, gates[1:2, :], 0.0
    )
    meta[0:8, :] = slot
    meta[8:16, :] = gate
    eye = lax.broadcasted_iota(jnp.int32, (count, count), 0) == lax.broadcasted_iota(
        jnp.int32, (count, count), 1
    )
    turned = lax.dot_general(
        jnp.where(eye, 1.0, 0.0).astype(BF16),
        meta[...].astype(BF16),
        (((1,), (1,)), ((), ())),
        preferred_element_type=F32,
    )
    index = lax.broadcasted_iota(jnp.int32, (count, capacity), 1).astype(F32)
    half = capacity // 2
    early = lax.broadcasted_iota(jnp.int32, (count, half), 1).astype(F32)

    def spread(k, slots):
        return jnp.where(
            turned[:, k : k + 1] == slots, turned[:, 8 + k : 9 + k], 0.0
        ).astype(BF16)

    two = spread(3, index)
    own_ref[...] = spread(0, index)
    plus_ref[...] = spread(1, index)
    one_ref[...] = spread(2, early)
    two_ref[...] = spread(2, early + half)
    for start in range(0, width, 512):
        cut = slice(start, start + 512)
        sum_ref[:, cut] = (
            rows_ref[:, cut].astype(F32)
            + jnp.dot(two, t_ref[:, cut], preferred_element_type=F32)
        )


def last_kernel(
    sum_ref, own_ref, plus_ref, one_ref, two_ref, same_ref, core_ref, other_ref,
    p_ref, m1_ref, m2_ref, out_ref,
):
    capacity = other_ref.shape[0]
    for start in range(0, sum_ref.shape[1], 512):
        cut = slice(start, start + 512)
        local_rows = (
            same_ref[:, cut] + core_ref[:capacity, cut].astype(F32) + other_ref[:, cut].astype(F32)
        ).astype(BF16)
        out_ref[0, :, cut] = (
            sum_ref[:, cut]
            + jnp.dot(own_ref[...], local_rows, preferred_element_type=F32)
            + jnp.dot(plus_ref[...], p_ref[:, cut], preferred_element_type=F32)
            + jnp.dot(one_ref[...], m1_ref[:, cut], preferred_element_type=F32)
            + jnp.dot(two_ref[...], m2_ref[:, cut], preferred_element_type=F32)
        ).astype(BF16)


def local(activations, expert_ids, gate_values, norm_gain, inner_weight, outer_weight):
    sections = lax.axis_size("section")
    owners = lax.axis_size("expert")
    rows = activations[0]
    count, width = rows.shape
    experts = owners // SPLIT
    capacity = min(count, 3 * count // experts)
    hidden_width = inner_weight.shape[-1]
    where = jnp.stack([lax.axis_index("section"), lax.axis_index("expert") // SPLIT])
    ids = jnp.swapaxes(expert_ids[0], 1, 2)
    gates = jnp.swapaxes(gate_values[0], 1, 2)

    def shape(size, kind=BF16, columns=width):
        return jax.ShapeDtypeStruct((size, columns), kind)

    def move(value, target):
        return lax.ppermute(value, "expert", [(i, target(i)) for i in range(owners)])

    def core(value):
        return move(value, lambda i: i ^ 1)

    def side(value):
        return move(value, lambda i: i ^ 2)

    def along(value, offset):
        return move(value, lambda i: (i + SPLIT * offset) % owners)

    tokens, *slots = call(
        functools.partial(front_kernel, capacity),
        (shape(count + 8),) + (shape(capacity),) * 4,
        where, rows, norm_gain, ids, gates,
        smem=1,
        hbm=4,
        scratch=[
            pltpu.VMEM((4 * capacity, count), BF16),
            pltpu.VMEM((count, width), BF16),
            pltpu.VMEM(norm_gain.shape, F32),
            pltpu.VMEM(ids.shape, jnp.int32),
            pltpu.VMEM(gates.shape, BF16),
            pltpu.VMEM((8, count), F32),
            pltpu.SemaphoreType.DMA((4,)),
        ],
    )
    first, second = call(
        load_kernel,
        (shape(width, columns=hidden_width), shape(hidden_width)),
        inner_weight[0, 0], outer_weight[0, 0],
        hbm=2,
        scratch=[pltpu.SemaphoreType.DMA((2, 4))],
    )
    o_slots, p_slots, m_slots, t_slots = slots
    others = side(tokens)
    o_cross, p_cross, m_cross = call(
        functools.partial(cross_kernel, capacity),
        (shape(capacity),) * 3,
        where, others,
        smem=1,
        scratch=[pltpu.VMEM((3 * capacity, count), BF16)],
    )

    def experts_of(one, two):
        hidden = call(
            inner_kernel,
            shape(4 * capacity, columns=hidden_width),
            one, two, core(one), core(two), first,
            scratch=[pltpu.VMEM((4 * capacity, width), BF16)],
            flops=8 * capacity * width * hidden_width,
        )
        same, across, send = call(
            outer_kernel,
            (shape(capacity, F32), shape(capacity, F32), shape(2 * capacity)),
            hidden, second,
            flops=8 * capacity * width * hidden_width,
        )
        return same, across, core(send)

    two_on = along(t_slots, 2)
    same, across, back = experts_of(two_on, side(two_on))
    got = side(call(side_kernel, shape(capacity), across, back))
    t_back = along(call(same_kernel, shape(capacity), same, back, got), -2)

    same_s, minus_s, back_s = experts_of(along(p_slots, 1), along(m_slots, -1))
    parts = experts_of(along(p_cross, 1), along(m_cross, -1))
    half = capacity // 2
    give_p, *give_m = call(cross_sums_kernel, (shape(capacity), shape(half), shape(half)), *parts)
    p_back = along(call(same_kernel, shape(capacity), same_s, back_s, side(give_p)), -1)
    m_back = [
        along(
            call(
                functools.partial(minus_half_kernel, k * half),
                shape(half),
                minus_s, back_s, side(give),
            ),
            1,
        )
        for k, give in enumerate(give_m)
    ]

    same, across, back = experts_of(o_slots, o_cross)
    got = side(call(side_kernel, shape(capacity), across, back))
    partial, *spreads = call(
        functools.partial(own_kernel, capacity),
        (
            shape(count, F32), shape(count, BF16, capacity), shape(count, BF16, capacity),
            shape(count, BF16, half), shape(count, BF16, half),
        ),
        where, rows, ids, gates, t_back,
        smem=1,
        scratch=[pltpu.VMEM((16, count), F32)],
    )
    layer_out = call(
        last_kernel,
        jax.ShapeDtypeStruct((1, count, width), BF16),
        partial, *spreads, same, back, got, p_back, *m_back,
    )
    return lax.ppermute(layer_out, "section", [(i, (i + 1) % sections) for i in range(sections)])


def solution(mesh):
    placed = (
        P("section", "expert", None),
        P("section", None, "expert", None),
        P("section", None, "expert", None),
        P("section", None),
        P("section", "expert", None, None),
        P("section", "expert", None, None),
    )
    return jax.shard_map(
        local, mesh=mesh, in_specs=placed, out_specs=P("section", "expert", None), check_vma=False
    )
```

```python
import functools

import jax
import jax.numpy as jnp
from jax import lax
from jax.experimental import pallas as pl
from jax.experimental.pallas import tpu as pltpu
from jax.sharding import PartitionSpec as P


SPLIT = 4
EPSILON = 1e-05
OFFSETS = (0, 1, 3, 2)
NAMES = ("o", "p", "m", "t")
BF16 = jnp.bfloat16
F32 = jnp.float32


VMEM = pl.BlockSpec(memory_space=pltpu.VMEM)
SMEM = pl.BlockSpec(memory_space=pltpu.SMEM)
HBM = pl.BlockSpec(memory_space=pltpu.HBM)


def call(kernel, out, *args, scratch=(), smem=0, hbm=0, limit=10, flops=0):
    args = [
        pltpu.with_memory_space_constraint(arg, pltpu.HBM) if smem <= k < smem + hbm else arg
        for k, arg in enumerate(args)
    ]
    return pl.pallas_call(
        kernel,
        out_shape=out,
        in_specs=[SMEM] * smem + [HBM] * hbm + [VMEM] * (len(args) - smem - hbm),
        out_specs=jax.tree.map(lambda _: VMEM, out),
        scratch_shapes=scratch,
        compiler_params=pltpu.CompilerParams(vmem_limit_bytes=limit * 2**20),
        cost_estimate=pl.CostEstimate(
            flops=flops, bytes_accessed=1 << 20, transcendentals=0
        ),
    )(*args)


def ranks(ids, here):
    count = ids.shape[1]
    row = lax.broadcasted_iota(jnp.int32, (8, count), 0)
    offset = jnp.where(row == 2, 3, jnp.where(row == 3, 2, row))
    expert = jnp.where(row < 4, (here + offset) % 4, -1)
    named = (ids[0:1, :] == expert) | (ids[1:2, :] == expert)
    member = jnp.where(named, 1.0, 0.0).astype(BF16)
    earlier = lax.broadcasted_iota(jnp.int32, (count, count), 0) <= lax.broadcasted_iota(
        jnp.int32, (count, count), 1
    )
    upto = jnp.dot(member, jnp.where(earlier, 1.0, 0.0).astype(BF16), preferred_element_type=F32)
    return expert, jnp.where(named, upto - 1.0, -1.0)


def load_kernel(first_hbm, second_hbm, first_ref, second_ref, sems):
    copies = []
    for k, (source, target) in enumerate(((first_hbm, first_ref), (second_hbm, second_ref))):
        size = source.shape[0] // 4
        for j in range(4):
            cut = pl.ds(j * size, size)
            copies.append(pltpu.make_async_copy(source.at[cut], target.at[cut], sems.at[k, j]))
    for copy in copies:
        copy.start()
    for copy in copies:
        copy.wait()


def front_kernel(capacity, where_ref, rows_hbm, gain_hbm, ids_hbm, *refs):
    outs, (normed, pick, rows_ref, gain_ref, ids_ref, sems) = refs[:4], refs[4:]
    copies = [
        pltpu.make_async_copy(ids_hbm, ids_ref, sems.at[0]),
        pltpu.make_async_copy(rows_hbm, rows_ref, sems.at[1]),
        pltpu.make_async_copy(gain_hbm, gain_ref, sems.at[2]),
    ]
    for copy in copies:
        copy.start()
    copies[0].wait()
    count, width = rows_ref.shape
    _, slot = ranks(ids_ref[where_ref[0]], where_ref[1])
    index = lax.broadcasted_iota(jnp.int32, (capacity, count), 0).astype(F32)
    for k in range(4):
        pick[k * capacity : (k + 1) * capacity, :] = jnp.where(
            slot[k : k + 1, :] == index, 1.0, 0.0
        ).astype(BF16)
    copies[1].wait()
    copies[2].wait()
    for start in range(0, count, 16):
        part = rows_ref[start : start + 16, :].astype(F32)
        centred = part - jnp.mean(part, axis=-1, keepdims=True)
        spread = jnp.mean(centred * centred, axis=-1, keepdims=True)
        normed[start : start + 16, :] = (
            centred * lax.rsqrt(spread + EPSILON) * gain_ref[...]
        ).astype(BF16)
    for start in range(0, width, 512):
        part = jnp.dot(pick[...], normed[:, start : start + 512], preferred_element_type=F32)
        for k in range(4):
            outs[k][:, start : start + 512] = part[k * capacity : (k + 1) * capacity].astype(BF16)


def inner_kernel(a_ref, b_ref, c_ref, d_ref, weight_ref, hidden_ref, gathered):
    size = a_ref.shape[0]
    for k, ref in enumerate((a_ref, b_ref, c_ref, d_ref)):
        gathered[k * size : (k + 1) * size, :] = ref[...]
    for start in range(0, weight_ref.shape[1], 512):
        part = jnp.dot(
            gathered[...], weight_ref[:, start : start + 512], preferred_element_type=F32
        )
        hidden_ref[:, start : start + 512] = jnp.maximum(part, 0.0).astype(BF16)


def outer_kernel(hidden_ref, weight_ref, same_ref, side_ref, send_ref):
    size = same_ref.shape[0]
    for start in range(0, weight_ref.shape[1], 512):
        part = jnp.dot(
            hidden_ref[...], weight_ref[:, start : start + 512], preferred_element_type=F32
        )
        same_ref[:, start : start + 512] = part[:size]
        side_ref[:, start : start + 512] = part[size : 2 * size]
        send_ref[:, start : start + 512] = part[2 * size :].astype(BF16)


def side_kernel(side_ref, core_ref, out_ref):
    size = side_ref.shape[0]
    out_ref[...] = (side_ref[...] + core_ref[size:, :].astype(F32)).astype(BF16)


def same_kernel(same_ref, core_ref, other_ref, out_ref):
    size = same_ref.shape[0]
    out_ref[...] = (
        same_ref[...] + core_ref[:size, :].astype(F32) + other_ref[...].astype(F32)
    ).astype(BF16)


def side_halves_kernel(side_ref, core_ref, *out_refs):
    size = side_ref.shape[0]
    half = size // 2
    for k, out_ref in enumerate(out_refs):
        cut = slice(k * half, (k + 1) * half)
        above = slice(size + k * half, size + (k + 1) * half)
        out_ref[...] = (side_ref[cut, :] + core_ref[above, :].astype(F32)).astype(BF16)


def same_half_kernel(base, same_ref, core_ref, other_ref, out_ref):
    cut = slice(base, base + other_ref.shape[0])
    out_ref[...] = (
        same_ref[cut, :] + core_ref[cut, :].astype(F32) + other_ref[...].astype(F32)
    ).astype(BF16)


def own_kernel(
    capacity, where_ref, rows_ref, ids_ref, gates_ref, p_ref, t_ref,
    sum_ref, own_ref, one_ref, two_ref, meta,
):
    count, width = rows_ref.shape
    ids = ids_ref[where_ref[0]]
    gates = gates_ref[where_ref[0]].astype(F32)
    expert, slot = ranks(ids, where_ref[1])
    gate = jnp.where(ids[0:1, :] == expert, gates[0:1, :], 0.0) + jnp.where(
        ids[1:2, :] == expert, gates[1:2, :], 0.0
    )
    meta[0:8, :] = slot
    meta[8:16, :] = gate
    eye = lax.broadcasted_iota(jnp.int32, (count, count), 0) == lax.broadcasted_iota(
        jnp.int32, (count, count), 1
    )
    turned = lax.dot_general(
        jnp.where(eye, 1.0, 0.0).astype(BF16),
        meta[...].astype(BF16),
        (((1,), (1,)), ((), ())),
        preferred_element_type=F32,
    )
    index = lax.broadcasted_iota(jnp.int32, (count, capacity), 1).astype(F32)
    half = capacity // 2
    early = lax.broadcasted_iota(jnp.int32, (count, half), 1).astype(F32)

    def spread(k, slots):
        return jnp.where(
            turned[:, k : k + 1] == slots, turned[:, 8 + k : 9 + k], 0.0
        ).astype(BF16)

    plus, two = spread(1, index), spread(3, index)
    own_ref[...] = spread(0, index)
    one_ref[...] = spread(2, early)
    two_ref[...] = spread(2, early + half)
    for start in range(0, width, 512):
        cut = slice(start, start + 512)
        sum_ref[:, cut] = (
            rows_ref[:, cut].astype(F32)
            + jnp.dot(plus, p_ref[:, cut], preferred_element_type=F32)
            + jnp.dot(two, t_ref[:, cut], preferred_element_type=F32)
        )


def last_kernel(
    sum_ref, own_ref, one_ref, two_ref, same_ref, core_ref, other_ref, m1_ref, m2_ref, out_ref
):
    capacity = other_ref.shape[0]
    for start in range(0, sum_ref.shape[1], 512):
        cut = slice(start, start + 512)
        local_rows = (
            same_ref[:, cut] + core_ref[:capacity, cut].astype(F32) + other_ref[:, cut].astype(F32)
        ).astype(BF16)
        out_ref[0, :, cut] = (
            sum_ref[:, cut]
            + jnp.dot(own_ref[...], local_rows, preferred_element_type=F32)
            + jnp.dot(one_ref[...], m1_ref[:, cut], preferred_element_type=F32)
            + jnp.dot(two_ref[...], m2_ref[:, cut], preferred_element_type=F32)
        ).astype(BF16)


def local(activations, expert_ids, gate_values, norm_gain, inner_weight, outer_weight):
    sections = lax.axis_size("section")
    owners = lax.axis_size("expert")
    rows = activations[0]
    count, width = rows.shape
    experts = owners // SPLIT
    capacity = min(count, 3 * count // experts)
    hidden_width = inner_weight.shape[-1]
    where = jnp.stack([lax.axis_index("section"), lax.axis_index("expert") // SPLIT])
    ids = jnp.swapaxes(expert_ids[0], 1, 2)
    gates = jnp.swapaxes(gate_values[0], 1, 2)

    def shape(size, kind=BF16, columns=width):
        return jax.ShapeDtypeStruct((size, columns), kind)

    def move(value, target):
        return lax.ppermute(value, "expert", [(i, target(i)) for i in range(owners)])

    def core(value):
        return move(value, lambda i: i ^ 1)

    def side(value):
        return move(value, lambda i: i ^ 2)

    def along(value, offset):
        return move(value, lambda i: (i + SPLIT * offset) % owners)

    slots = call(
        functools.partial(front_kernel, capacity),
        (shape(capacity),) * 4,
        where, rows, norm_gain, ids,
        smem=1,
        hbm=3,
        scratch=[
            pltpu.VMEM((count, width), BF16),
            pltpu.VMEM((4 * capacity, count), BF16),
            pltpu.VMEM((count, width), BF16),
            pltpu.VMEM(norm_gain.shape, F32),
            pltpu.VMEM(ids.shape, jnp.int32),
            pltpu.SemaphoreType.DMA((3,)),
        ],
    )
    first, second = call(
        load_kernel,
        (shape(width, columns=hidden_width), shape(hidden_width)),
        inner_weight[0, 0], outer_weight[0, 0],
        hbm=2,
        scratch=[pltpu.SemaphoreType.DMA((2, 4))],
    )
    kept = {}
    for name, offset, slot in zip(NAMES, OFFSETS, slots):
        mine = slot if offset == 0 else along(slot, offset)
        other = side(mine)
        hidden = call(
            inner_kernel,
            shape(4 * capacity, columns=hidden_width),
            mine, other, core(mine), core(other), first,
            scratch=[pltpu.VMEM((4 * capacity, width), BF16)],
            flops=8 * capacity * width * hidden_width,
        )
        same, across, send = call(
            outer_kernel,
            (shape(capacity, F32), shape(capacity, F32), shape(2 * capacity)),
            hidden, second,
            flops=8 * capacity * width * hidden_width,
        )
        back = core(send)
        if name == "m":
            half = capacity // 2
            gives = call(side_halves_kernel, (shape(half),) * 2, across, back)
            kept[name] = [
                along(
                    call(
                        functools.partial(same_half_kernel, k * half),
                        shape(half),
                        same, back, side(give),
                    ),
                    -offset,
                )
                for k, give in enumerate(gives)
            ]
            continue
        got = side(call(side_kernel, shape(capacity), across, back))
        if name == "o":
            kept[name] = (same, back, got)
        else:
            total = call(same_kernel, shape(capacity), same, back, got)
            kept[name] = along(total, -offset)
    partial, *spreads = call(
        functools.partial(own_kernel, capacity),
        (
            shape(count, F32), shape(count, BF16, capacity),
            shape(count, BF16, capacity // 2), shape(count, BF16, capacity // 2),
        ),
        where, rows, ids, gates, kept["p"], kept["t"],
        smem=1,
        scratch=[pltpu.VMEM((16, count), F32)],
    )
    layer_out = call(
        last_kernel,
        jax.ShapeDtypeStruct((1, count, width), BF16),
        partial, *spreads, *kept["o"], *kept["m"],
    )
    moved = lax.ppermute(layer_out, "section", [(i, (i + 1) % sections) for i in range(sections)])
    return moved


def solution(mesh):
    placed = (
        P("section", "expert", None),
        P("section", None, "expert", None),
        P("section", None, "expert", None),
        P("section", None),
        P("section", "expert", None, None),
        P("section", "expert", None, None),
    )
    return jax.shard_map(
        local, mesh=mesh, in_specs=placed, out_specs=P("section", "expert", None), check_vma=False
    )
```
